32 devices in a mesh: row: 4 (over x, core), col: 8 (over z, y).
Axes of the slice: x: 2, y: 2, z: 4, core: 2. Of those that a mesh axis runs over, the one named last changes fastest.
Arguments:
- velocity: float32 [3, 2, 128, 512, 256], P(None, None, 'row', 'col'), may hold values from -6 to 6
- register: float32 [3, 2, 128, 512, 256], P(None, None, 'row', 'col'), may hold values from -6 to 6
- offsets: int32 [256], replicated, may hold values from -2 to 2, as said below
- remesh_flag: int32 [256], replicated, may hold values from 0 to 1, as said below
- keep_blocks: int32 [8], replicated, may hold values 0 or 1
Outputs:
- velocity_next: float32 [3, 2, 128, 512, 256], P(None, None, 'row', 'col')
The draws below stay inside these ranges and needn't reach their ends.
Inputs may be any that keep to these rules, and one draw needn't show every extreme that they name: offsets[j] is 0 or has the sign of ky = j - 128. On each side of ky = 0 the planes of magnitude 1 form one run of consecutive ky, and the planes of magnitude 2 the run that follows it directly, farther from ky = 0. Each of -2, -1, 1 and 2 is carried by half of 32 to 32 planes. Each nonzero value of offsets[j] remesh_flag[j] is taken by at most 32 planes, and in every draw one of them by exactly 32 planes.
All inputs are finite; a program needn't handle non-finite values.
Results may differ from the reference program's by a relative error of at most 0.0055.
Values may be sent and summed in bfloat16 or wider, within the bound.
A program may use at most 192 MiB of HBM per device.

```python
import math
import jax
import jax.numpy as jnp
from jax import lax

NX = 512
NY = 256
NZ = 256
NZH = 128
MX = 768
MY = 384
MZ = 384
KXB = 64
NBLK = 8
SHIFT_CAP = 32


def remesh_plan(key):
    folded = jax.random.fold_in(key, 4721)
    key_counts, key_pick, key_upper, key_lower, key_flag = jax.random.split(folded, 5)
    counts = jax.random.randint(key_counts, (4,), SHIFT_CAP // 2, SHIFT_CAP + 1).astype(jnp.int32)
    chosen = jax.random.randint(key_pick, (), 0, 4).astype(jnp.int32)
    slot_order = jnp.arange(4, dtype=jnp.int32)
    counts = jnp.where(slot_order == chosen, SHIFT_CAP, counts).astype(jnp.int32)
    upper_start = jax.random.randint(key_upper, (), 1, NY // 2 - counts[2] - counts[3] + 1).astype(jnp.int32)
    lower_start = jax.random.randint(key_lower, (), 1, NY // 2 - counts[1] - counts[0] + 2).astype(jnp.int32)
    ky_values = jnp.arange(NY, dtype=jnp.int32) - NY // 2
    upper_one = (ky_values >= upper_start) & (ky_values < upper_start + counts[2])
    upper_two = (ky_values >= upper_start + counts[2]) & (ky_values < upper_start + counts[2] + counts[3])
    lower_one = (ky_values <= -lower_start) & (ky_values > -lower_start - counts[1])
    lower_two = (ky_values <= -lower_start - counts[1]) & (ky_values > -lower_start - counts[1] - counts[0])
    offsets = (upper_one.astype(jnp.int32) + 2 * upper_two.astype(jnp.int32) - lower_one.astype(jnp.int32) - 2 * lower_two.astype(jnp.int32)).astype(jnp.int32)
    values = jnp.array([-2, -1, 1, 2], dtype=jnp.int32)
    chosen_value = jnp.sum(jnp.where(slot_order == chosen, values, 0)).astype(jnp.int32)
    coins = jax.random.randint(key_flag, (NY,), 0, 4).astype(jnp.int32)
    flag = jnp.where(offsets == chosen_value, 1, jnp.where(offsets != 0, (coins < 3).astype(jnp.int32), (coins < 2).astype(jnp.int32))).astype(jnp.int32)
    return (offsets, flag)


def draw_offsets(key, part):
    return remesh_plan(key)[0]


def draw_remesh_flag(key, part):
    return remesh_plan(key)[1]


def place_ends(result, stream_key, low, top_value):
    shape = result.shape
    place = [jax.random.randint(jax.random.fold_in(stream_key, axis), (), 0, shape[axis]) for axis in range(len(shape))]
    result = result.at[tuple(place)].set(low)
    longest = shape.index(max(shape))
    place[longest] = (place[longest] + 1) % shape[longest]
    return result.at[tuple(place)].set(top_value)


def level_of(own_key, extent, cuts, low, high):
    loudness, own = 1.0, jax.random.fold_in(own_key, 6)
    for axis_at, blocks in cuts:
        draws = jnp.exp(jax.random.uniform(jax.random.fold_in(own, axis_at), (blocks,), jnp.float32, low / len(cuts), high / len(cuts)))
        loudness = loudness * jnp.repeat(draws, extent[axis_at] // blocks).reshape([-1 if axis == axis_at else 1 for axis in range(len(extent))])
    return loudness


def normal_values(rng, shape, spread, most, cuts=(), kind=jnp.bfloat16):
    entries = jax.random.normal(rng, shape, jnp.float32) * spread
    if len(cuts) > 0:
        entries = level_of(rng, shape, cuts, -0.22, 0.18) * entries
    return jnp.clip(entries, min=-most, max=most).astype(kind)


def setup_inputs(seed: int = 0) -> dict:
    splits = jax.random.split(jax.random.key(seed), 6)
    return {
        "velocity": normal_values(splits[0], (3, 2, NZH, NX, NY), 1.0, 6.0, ((2, 4), (3, 8)), jnp.float32),
        "register": normal_values(splits[1], (3, 2, NZH, NX, NY), 1.0, 6.0, ((2, 4), (3, 8)), jnp.float32),
        "offsets": draw_offsets(jax.random.fold_in(splits[5], 71), 0),
        "remesh_flag": draw_remesh_flag(jax.random.fold_in(splits[5], 71), 0),
        "keep_blocks": place_ends((jax.random.randint(splits[4], (NBLK,), 0, 4) < 3).astype(jnp.int32), jax.random.fold_in(splits[4], 1), 0, 1),
    }


SHEAR_RATE = 40.0
SHEAR_TIME = 0.3
VISCOSITY = 0.0015
TIME_STEP = 0.008
REGISTER_WEIGHT = -153.0 / 128.0
UPDATE_WEIGHT = 8.0 / 15.0
PRODUCT_PAIRS = ((0, 0), (0, 1), (0, 2), (1, 1), (1, 2), (2, 2))
PAIR_LOOKUP = ((0, 1, 2), (1, 3, 4), (2, 4, 5))
OFFSET_VALUES = (-2, -1, 1, 2)
slab_rows = 32
kz_rows = 8

def phase_angles(contracted, produced, period):
    phase_turns = jnp.mod(contracted[:, None] * produced[None, :], period)
    return phase_turns.astype(jnp.float32) * (2.0 * math.pi / period)

def complex_table(contracted, produced, period, direction):
    angles = phase_angles(contracted, produced, period)
    cosine = jnp.cos(angles)
    sine_part = direction * jnp.sin(angles)
    upper_rows = jnp.stack([cosine, sine_part], axis=1)
    lower_rows = jnp.stack([-sine_part, cosine], axis=1)
    return jnp.stack([upper_rows, lower_rows], axis=0).astype(jnp.bfloat16)

def inverse_real_table(mode_list, points, period):
    angles = phase_angles(mode_list, points, period)
    weights = jnp.where(mode_list == 0, 1.0, 2.0).astype(jnp.float32)[:, None]
    return jnp.stack([weights * jnp.cos(angles), -weights * jnp.sin(angles)], axis=0).astype(jnp.bfloat16)

def forward_real_table(points, mode_list, period):
    angles = phase_angles(points, mode_list, period)
    return jnp.stack([jnp.cos(angles), -jnp.sin(angles)], axis=1).astype(jnp.bfloat16)

def tendency_update(spectra, velocity, register, kx_values, ky_values, kz_values):
    wave_x = kx_values[None, :, None] - SHEAR_TIME * ky_values[None, None, :]
    wave_y = ky_values[None, None, :]
    wave_z = kz_values[:, None, None]
    wave_list = (wave_x, wave_y, wave_z)
    squared = wave_x * wave_x + wave_y * wave_y + wave_z * wave_z
    inverse = 1.0 / jnp.maximum(squared, 1.0)
    advect_real = [sum((wave_list[source] * spectra[PAIR_LOOKUP[target][source], 1] for source in range(3))) for target in range(3)]
    advect_imag = [-sum((wave_list[source] * spectra[PAIR_LOOKUP[target][source], 0] for source in range(3))) for target in range(3)]
    diverge_real = sum((wave_list[target] * advect_real[target] for target in range(3)))
    diverge_imag = sum((wave_list[target] * advect_imag[target] for target in range(3)))
    pressure_lift = 2.0 * SHEAR_RATE * wave_y * inverse
    results = []
    for target in range(3):
        halves = []
        for half_index, advect, diverge in ((0, advect_real, diverge_real), (1, advect_imag, diverge_imag)):
            rate_value = advect[target] - wave_list[target] * diverge * inverse
            rate_value = rate_value + wave_list[target] * pressure_lift * velocity[0, half_index]
            rate_value = rate_value - VISCOSITY * squared * velocity[target, half_index]
            if target == 1:
                rate_value = rate_value - SHEAR_RATE * velocity[0, half_index]
            increment = REGISTER_WEIGHT * register[target, half_index] + TIME_STEP * rate_value
            halves.append(velocity[target, half_index] + UPDATE_WEIGHT * increment)
        results.append(jnp.stack(halves))
    return jnp.stack(results)

def contract(formula, left_operand, right_operand):
    return jnp.einsum(formula, left_operand.astype(jnp.float32), right_operand.astype(jnp.float32), precision=lax.Precision.HIGHEST)

def reference(velocity, register, offsets, remesh_flag, keep_blocks):
    inverse_scale = 1.0 / math.sqrt(NX * NY * NZ)
    forward_scale = math.sqrt(NX * NY * NZ) / (MX * MY * MZ)
    kx_all = jnp.arange(NX, dtype=jnp.int32) - NX // 2
    ky_all = jnp.arange(NY, dtype=jnp.int32) - NY // 2
    kz_all = jnp.arange(NZH, dtype=jnp.int32)
    x_points = jnp.arange(MX, dtype=jnp.int32)
    y_points = jnp.arange(MY, dtype=jnp.int32)
    z_points = jnp.arange(MZ, dtype=jnp.int32)
    y_inverse = complex_table(ky_all, y_points, MY, 1.0)
    x_inverse = complex_table(kx_all, x_points, MX, 1.0)
    z_inverse = inverse_real_table(kz_all, z_points, MZ)
    z_forward = forward_real_table(z_points, kz_all, MZ)
    x_forward = complex_table(x_points, kx_all, MX, -1.0)
    y_forward = complex_table(y_points, ky_all, MY, -1.0)
    collected = []
    for component in range(3):
        spectral = velocity[component].astype(jnp.bfloat16)
        along_y = contract('rlij,rjsq->slqi', spectral, y_inverse).astype(jnp.bfloat16)
        collected.append(contract('rlqi,risp->slqp', along_y, x_inverse).astype(jnp.bfloat16))
    grids = jnp.stack(collected)

    def slab_products(start):
        section = lax.dynamic_slice_in_dim(grids, start, slab_rows, 3)
        fields = contract('crlqp,rlz->cqpz', section, z_inverse) * inverse_scale
        products = jnp.stack([fields[left_factor] * fields[right_factor] for left_factor, right_factor in PRODUCT_PAIRS]).astype(jnp.bfloat16)
        modes_z = contract('eqpz,zsl->esqpl', products, z_forward).astype(jnp.bfloat16)
        return contract('erqpl,rpsi->esqil', modes_z, x_forward).astype(jnp.bfloat16)
    slabs = lax.map(slab_products, jnp.arange(MY // slab_rows, dtype=jnp.int32) * slab_rows)
    modes_x = jnp.moveaxis(slabs, 0, 2).reshape(6, 2, MY, NX, NZH)

    def kz_update(start):
        section = lax.dynamic_slice_in_dim(modes_x, start, kz_rows, 4)
        spectra = contract('erqil,rqsj->eslij', section, y_forward) * forward_scale
        velocity_part = lax.dynamic_slice_in_dim(velocity, start, kz_rows, 2)
        register_part = lax.dynamic_slice_in_dim(register, start, kz_rows, 2)
        kz_values = (start + jnp.arange(kz_rows, dtype=jnp.int32)).astype(jnp.float32)
        return tendency_update(spectra, velocity_part, register_part, kx_all.astype(jnp.float32), ky_all.astype(jnp.float32), kz_values)
    updates = lax.map(kz_update, jnp.arange(NZH // kz_rows, dtype=jnp.int32) * kz_rows)
    updated = jnp.moveaxis(updates, 0, 2).reshape(3, 2, NZH, NX, NY)
    moved_by = offsets * remesh_flag
    remeshed = updated * (moved_by == 0).astype(jnp.float32)
    for shift_by in OFFSET_VALUES:
        selected = updated * (moved_by == shift_by).astype(jnp.float32)
        amount = shift_by * KXB
        if amount > 0:
            selected = jnp.pad(selected[:, :, :, :NX - amount], ((0, 0), (0, 0), (0, 0), (amount, 0), (0, 0)))
        else:
            selected = jnp.pad(selected[:, :, :, -amount:], ((0, 0), (0, 0), (0, 0), (0, -amount), (0, 0)))
        remeshed = remeshed + selected
    block_keep = keep_blocks[jnp.arange(NX, dtype=jnp.int32) // KXB].astype(jnp.float32)
    return remeshed * block_keep[None, None, None, :, None]
```

```python
import functools
import math

import jax
import jax.numpy as jnp
from jax import lax
from jax.experimental import pallas as pl
from jax.experimental.pallas import tpu as pltpu
from jax.sharding import PartitionSpec as P

SHEAR_RATE = 40.0
SHEAR_TIME = 0.3
VISCOSITY = 0.0015
TIME_STEP = 0.008
REGISTER_WEIGHT = -153.0 / 128.0
UPDATE_WEIGHT = 8.0 / 15.0
OFFSET_VALUES = (-2, -1, 1, 2)
SHIFT_CAP = 32
SENT_PRODUCTS = 5
CHUNKS = 2
VMEM_LIMIT = 60 * 1024 * 1024


def from_behind(block, axis, distance):
    devices = range(lax.axis_size(axis))
    route = [(i - distance, i) for i in devices if i - distance in devices]
    return lax.ppermute(block, axis, route)


def cosine_turns(turns, period):
    turns = jnp.mod(turns, period)
    return jnp.cos(turns.astype(jnp.float32) * (2.0 * math.pi / period))


def split_rows(count, parts):
    base = count // parts
    sizes = [base + (1 if k >= parts - count % parts else 0) for k in range(parts)]
    return [s for s in sizes if s > 0]


def call(body, grid, in_specs, out_specs, out_shape, scratch=(), flops=0, moved=0, name=None):
    return pl.pallas_call(
        body,
        grid=grid,
        in_specs=in_specs,
        out_specs=out_specs,
        out_shape=out_shape,
        scratch_shapes=list(scratch),
        compiler_params=pltpu.CompilerParams(vmem_limit_bytes=VMEM_LIMIT),
        cost_estimate=pl.CostEstimate(flops=flops, bytes_accessed=moved, transcendentals=0),
        name=name,
    )


def y_inverse_body(table_ref, velocity_ref, out_ref, hold):
    slabs = velocity_ref.shape[2]
    for l in range(slabs):
        real = velocity_ref[0, 0, l].astype(jnp.bfloat16)
        imag = velocity_ref[0, 1, l].astype(jnp.bfloat16)
        straight = jnp.concatenate([real, imag], axis=0)
        turned = jnp.concatenate([-imag, real], axis=0)
        both = jnp.concatenate([straight, turned], axis=1)
        hold[l] = lax.dot_general(
            table_ref[...], both, (((1,), (1,)), ((), ())), preferred_element_type=jnp.float32
        )
    for d in range(out_ref.shape[0]):
        count = out_ref.shape[2]
        piece = hold[:, d * count : (d + 1) * count, :]
        out_ref[d, 0] = jnp.swapaxes(piece, 0, 1).astype(jnp.bfloat16)


def y_inverse(velocity, table, devices, slab_y):
    comps, _, kz, kx, ky = velocity.shape
    block = min(16, kz)
    return call(
        y_inverse_body,
        (comps, kz // block),
        [
            pl.BlockSpec(table.shape, lambda c, l: (0, 0)),
            pl.BlockSpec((1, 2, block, kx, ky), lambda c, l: (c, 0, l, 0, 0)),
        ],
        pl.BlockSpec((devices, 1, slab_y, block, 2 * kx), lambda c, l: (0, c, 0, l, 0)),
        jax.ShapeDtypeStruct((devices, comps, slab_y, kz, 2 * kx), jnp.bfloat16),
        [pltpu.VMEM((block, devices * slab_y, 2 * kx), jnp.float32)],
        flops=8 * comps * kz * kx * ky * devices * slab_y,
        moved=velocity.size * 4 + devices * comps * slab_y * kz * kx * 4,
        name="y_inverse",
    )(table, velocity)


def grid_body(scale, in_ref, xi_ref, zi_ref, zf_ref, xf_ref, out_ref, rows_in, fields, rows_out):
    rows, cols, comps, _, kz, width = in_ref.shape
    modes = rows * kz
    for c in range(comps):
        for r in range(rows):
            for q in range(cols):
                rows_in[c * modes + r * kz : c * modes + (r + 1) * kz, q * width : (q + 1) * width] = (
                    in_ref[r, q, c, 0]
                )
    points = xi_ref.shape[1] // 2
    for c in range(comps):
        along = jnp.dot(
            rows_in[c * modes : (c + 1) * modes, :], xi_ref[...], preferred_element_type=jnp.float32
        ).astype(jnp.bfloat16)
        stacked = jnp.concatenate([along[:, :points], along[:, points:]], axis=0)
        fields[c] = jnp.dot(zi_ref[...], stacked, preferred_element_type=jnp.float32) * scale
    for e in range(out_ref.shape[2]):
        if e == 0:
            product = fields[0] * fields[0] - fields[2] * fields[2]
        elif e == 1:
            product = fields[0] * fields[1]
        elif e == 2:
            product = fields[0] * fields[2]
        elif e == 3:
            product = fields[1] * fields[1] - fields[2] * fields[2]
        else:
            product = fields[1] * fields[2]
        modes_z = jnp.dot(
            zf_ref[...], product.astype(jnp.bfloat16), preferred_element_type=jnp.float32
        ).astype(jnp.bfloat16)
        rows_out[:, :points] = modes_z[:modes]
        rows_out[:, points:] = modes_z[modes:]
        result = jnp.dot(rows_out[...], xf_ref[...], preferred_element_type=jnp.float32).astype(
            jnp.bfloat16
        )
        for r in range(rows):
            for q in range(cols):
                out_ref[r, q, e, 0] = result[r * kz : (r + 1) * kz, q * width : (q + 1) * width]


def grid_stage(arrived, xi, zi, zf, xf, scale):
    rows, cols, comps, slab_y, kz, width = arrived.shape
    modes, points, deep = rows * kz, xi.shape[1] // 2, zi.shape[0]
    whole = lambda table: pl.BlockSpec(
        table.shape, lambda y: (0, 0), pipeline_mode=pl.Buffered(1)
    )
    work = comps * modes * xi.size + comps * zi.size * points
    work += SENT_PRODUCTS * (zf.size * points + modes * xf.size)
    return call(
        functools.partial(grid_body, scale),
        (slab_y,),
        [
            pl.BlockSpec((rows, cols, comps, 1, kz, width), lambda y: (0, 0, 0, y, 0, 0)),
            whole(xi),
            whole(zi),
            whole(zf),
            whole(xf),
        ],
        pl.BlockSpec((rows, cols, SENT_PRODUCTS, 1, kz, width), lambda y: (0, 0, 0, y, 0, 0)),
        jax.ShapeDtypeStruct((rows, cols, SENT_PRODUCTS, slab_y, kz, width), jnp.bfloat16),
        [
            pltpu.VMEM((comps * modes, cols * width), jnp.bfloat16),
            pltpu.VMEM((comps, deep, points), jnp.float32),
            pltpu.VMEM((modes, 2 * points), jnp.bfloat16),
        ],
        flops=2 * slab_y * work,
        moved=arrived.size * 6,
        name="grid_stage",
    )(arrived, xi, zi, zf, xf)


def update_body(parts, scale, kz_block, *refs):
    gathered = refs[:parts]
    tables = refs[parts : 2 * parts]
    velocity_ref, register_ref, pick_ref, updated_ref, picked_ref, hold, spectra = refs[2 * parts :]
    _, _, slabs, kx, ky = velocity_ref.shape
    width = 2 * kx
    for e in range(SENT_PRODUCTS):
        for part in range(parts):
            source = gathered[part]
            devices, _, slab_y, _, _ = source.shape
            for d in range(devices):
                base = d * slab_y
                hold[part][:, base : base + slab_y, :] = jnp.swapaxes(
                    source[d, e].astype(jnp.float32), 0, 1
                )
        for l in range(slabs):
            total = None
            for part in range(parts):
                term = lax.dot_general(
                    hold[part][l].astype(jnp.bfloat16),
                    tables[part][...],
                    (((0,), (0,)), ((), ())),
                    preferred_element_type=jnp.float32,
                )
                total = term if total is None else total + term
            cos_part, sin_part = total[:, :ky], total[:, ky:]
            spectra[e, 0, l] = (cos_part[:kx] + sin_part[kx:]) * scale
            spectra[e, 1, l] = (cos_part[kx:] - sin_part[:kx]) * scale
    kx_first = (lax.axis_index("col") * kx - kx * lax.axis_size("col") // 2).astype(jnp.float32)
    kz_first = (lax.axis_index("row") * kz_block + pl.program_id(0) * slabs).astype(jnp.float32)
    k_y = lax.broadcasted_iota(jnp.int32, (kx, ky), 1).astype(jnp.float32) - float(ky // 2)
    k_x = lax.broadcasted_iota(jnp.int32, (kx, ky), 0).astype(jnp.float32) + kx_first
    k_x = k_x - SHEAR_TIME * k_y
    plane = k_x * k_x + k_y * k_y
    for l in range(slabs):
        k_z = kz_first + float(l)
        squared = plane + k_z * k_z
        inverse = 1.0 / jnp.maximum(squared, 1.0)
        waves = (k_x, k_y, k_z)
        lift = 2.0 * SHEAR_RATE * k_y * inverse
        for half in range(2):
            p = [spectra[e, 1 - half, l] for e in range(SENT_PRODUCTS)]
            advect = [
                k_x * p[0] + k_y * p[1] + k_z * p[2],
                k_x * p[1] + k_y * p[3] + k_z * p[4],
                k_x * p[2] + k_y * p[4],
            ]
            if half == 1:
                advect = [-value for value in advect]
            diverge = k_x * advect[0] + k_y * advect[1] + k_z * advect[2]
            first = velocity_ref[0, half, l]
            shared = lift * first - diverge * inverse
            for m in range(3):
                own = first if m == 0 else velocity_ref[m, half, l]
                rate = advect[m] + waves[m] * shared - VISCOSITY * squared * own
                if m == 1:
                    rate = rate - SHEAR_RATE * first
                increment = REGISTER_WEIGHT * register_ref[m, half, l] + TIME_STEP * rate
                updated_ref[m, half, l] = own + UPDATE_WEIGHT * increment
    for m in range(3):
        for half in range(2):
            rounded = updated_ref[m, half].astype(jnp.bfloat16).reshape(slabs * kx, ky)
            chosen = lax.dot_general(
                pick_ref[...], rounded, (((1,), (1,)), ((), ())), preferred_element_type=jnp.float32
            ).astype(jnp.bfloat16)
            for v in range(len(OFFSET_VALUES)):
                picked_ref[v, m, half] = chosen[v * SHIFT_CAP : (v + 1) * SHIFT_CAP]


def update_stage(gathered, tables, velocity, register, pick, scale):
    comps, _, kz, kx, ky = velocity.shape
    block = min(8, kz)
    parts = len(gathered)
    state = pl.BlockSpec((comps, 2, block, kx, ky), lambda l: (0, 0, l, 0, 0))
    shifts = len(OFFSET_VALUES)

    def body(*refs):
        inner = list(refs[: 2 * parts + 5])
        holds = refs[2 * parts + 5 : 3 * parts + 5]
        update_body(parts, scale, kz, *inner, holds, refs[-1])

    in_specs = [
        pl.BlockSpec(g.shape[:3] + (block, g.shape[4]), lambda l: (0, 0, 0, l, 0)) for g in gathered
    ]
    in_specs += [pl.BlockSpec(t.shape, lambda l: (0, 0), pipeline_mode=pl.Buffered(1)) for t in tables]
    in_specs += [state, state, pl.BlockSpec(pick.shape, lambda l: (0, 0))]
    return call(
        body,
        (kz // block,),
        in_specs,
        [
            state,
            pl.BlockSpec((shifts, comps, 2, SHIFT_CAP, block * kx), lambda l: (0, 0, 0, 0, l)),
        ],
        [
            jax.ShapeDtypeStruct(velocity.shape, jnp.float32),
            jax.ShapeDtypeStruct((shifts, comps, 2, SHIFT_CAP, kz * kx), jnp.bfloat16),
        ],
        [pltpu.VMEM((block, t.shape[0], 2 * kx), jnp.float32) for t in tables]
        + [pltpu.VMEM((SENT_PRODUCTS, 2, block, kx, ky), jnp.float32)],
        flops=1,
        moved=velocity.size * 16,
        name="update_stage",
    )(*gathered, *tables, velocity, register, pick)


def remesh_body(shifts, *refs):
    arrived = refs[:shifts]
    updated_ref, pick_ref, stay_ref, keep_ref, out_ref = refs[shifts:]
    comps, _, slabs, kx, ky = updated_ref.shape
    keep = keep_ref[...]
    stay = stay_ref[...] * keep
    for m in range(comps):
        for half in range(2):
            planes = jnp.concatenate([ref[m, half] for ref in arrived], axis=0)
            moved = lax.dot_general(
                planes, pick_ref[...], (((0,), (0,)), ((), ())), preferred_element_type=jnp.float32
            )
            own = updated_ref[m, half].reshape(slabs * kx, ky)
            out_ref[m, half] = (own * stay + moved * keep).reshape(slabs, kx, ky)


def remesh_stage(arrived, updated, pick, stay, keep):
    comps, _, kz, kx, ky = updated.shape
    block = min(8, kz)
    state = pl.BlockSpec((comps, 2, block, kx, ky), lambda l: (0, 0, l, 0, 0))
    planes = pl.BlockSpec((comps, 2, SHIFT_CAP, block * kx), lambda l: (0, 0, 0, l))
    row = pl.BlockSpec((1, ky), lambda l: (0, 0))
    return call(
        functools.partial(remesh_body, len(arrived)),
        (kz // block,),
        [planes] * len(arrived) + [state, pl.BlockSpec(pick.shape, lambda l: (0, 0)), row, row],
        state,
        jax.ShapeDtypeStruct(updated.shape, jnp.float32),
        flops=1,
        moved=updated.size * 10,
        name="remesh_stage",
    )(*arrived, updated, pick, stay, keep)


def local(velocity, register, offsets, remesh_flag, keep_blocks):
    rows = lax.axis_size("row")
    cols = lax.axis_size("col")
    col_index = lax.axis_index("col")
    devices = rows * cols
    comps, _, kz, kx, ny = velocity.shape
    nx, nzh = kx * cols, kz * rows
    nz = 2 * nzh
    mx, my, mz = nx * 3 // 2, ny * 3 // 2, nz * 3 // 2
    slab_y = my // devices
    inverse_scale = 1.0 / math.sqrt(nx * ny * nz)
    forward_scale = math.sqrt(nx * ny * nz) / (mx * my * mz)
    ky_all = jnp.arange(ny, dtype=jnp.int32) - ny // 2
    kz_all = jnp.arange(nzh, dtype=jnp.int32)

    sizes = split_rows(slab_y, CHUNKS)
    y_lists, start = [], 0
    for size in sizes:
        own = jnp.arange(devices, dtype=jnp.int32)[:, None] * slab_y + start
        y_lists.append((own + jnp.arange(size, dtype=jnp.int32)).reshape(-1))
        start += size
    inverse_tables, forward_tables = [], []
    for y_points in y_lists:
        turns = y_points[:, None] * ky_all[None, :]
        cosine = cosine_turns(turns, my)
        sine = cosine_turns(turns - my // 4, my)
        table = jnp.concatenate([cosine, sine], axis=1).astype(jnp.bfloat16)
        inverse_tables.append(table)
        forward_tables.append(table)

    split_index = jnp.arange(2 * nx, dtype=jnp.int32)
    part_kx = split_index // kx % 2
    wave_kx = split_index // (2 * kx) * kx + split_index % kx - nx // 2
    point_index = jnp.arange(2 * mx, dtype=jnp.int32)
    part_x, point_x = point_index // mx, point_index % mx
    turn_x = wave_kx[:, None] * point_x[None, :]
    quarter = part_kx[:, None] - part_x[None, :]
    xi = cosine_turns(turn_x + quarter * (mx // 4), mx).astype(jnp.bfloat16)
    turn_f = point_x[:, None] * wave_kx[None, :]
    quarter_f = part_kx[None, :] - part_x[:, None]
    xf = cosine_turns(turn_f + quarter_f * (mx // 4), mx).astype(jnp.bfloat16)
    z_points = jnp.arange(mz, dtype=jnp.int32)
    turn_z = z_points[:, None] * kz_all[None, :]
    weight = jnp.where(kz_all == 0, 1.0, 2.0).astype(jnp.float32)[None, :]
    cos_z, minus_sin_z = cosine_turns(turn_z, mz), cosine_turns(turn_z + mz // 4, mz)
    zi = jnp.concatenate([weight * cos_z, weight * minus_sin_z], axis=1).astype(jnp.bfloat16)
    zf = jnp.concatenate([cos_z.T, minus_sin_z.T], axis=0).astype(jnp.bfloat16)

    moved_by = offsets * remesh_flag
    picks = []
    for shift_by in OFFSET_VALUES:
        hit = moved_by == shift_by
        place = jnp.cumsum(hit.astype(jnp.int32)) - 1
        slots = jnp.arange(SHIFT_CAP, dtype=jnp.int32)[:, None]
        picks.append((slots == place[None, :]) & hit[None, :])
    pick = jnp.concatenate(picks, axis=0).astype(jnp.bfloat16)
    stay = (moved_by == 0).astype(jnp.float32)[None, :]
    keep_here = jnp.sum(
        jnp.where(jnp.arange(cols, dtype=jnp.int32) == col_index, keep_blocks, 0)
    ).astype(jnp.float32)
    keep = jnp.broadcast_to(keep_here, (1, ny))

    arrived = []
    for table, size in zip(inverse_tables, sizes):
        sent = y_inverse(velocity, table, devices, size)
        sent = lax.all_to_all(sent, ("row", "col"), split_axis=0, concat_axis=0, tiled=True)
        arrived.append(sent.reshape((rows, cols) + sent.shape[1:]))
    gathered = []
    for block in arrived:
        modes = grid_stage(block, xi, zi, zf, xf, inverse_scale)
        modes = modes.reshape((devices,) + modes.shape[2:])
        gathered.append(
            lax.all_to_all(modes, ("row", "col"), split_axis=0, concat_axis=0, tiled=True)
        )
    updated, picked = update_stage(
        gathered, forward_tables, velocity, register, pick, forward_scale
    )
    received = [from_behind(picked[v], "col", OFFSET_VALUES[v]) for v in range(len(OFFSET_VALUES))]
    return remesh_stage(received, updated, pick, stay, keep)


def solution(mesh):
    placed = (P(None, None, "row", "col", None), P(None, None, "row", "col", None), P(), P(), P())
    return jax.shard_map(
        local,
        mesh=mesh,
        in_specs=placed,
        out_specs=P(None, None, "row", "col", None),
        check_vma=False,
    )
```
